32 devices in a mesh: parts: 2 (over x), xline: 16 (over z, y, core).
Axes of the slice: x: 2, y: 2, z: 4, core: 2. Of those that a mesh axis runs over, the one named last changes fastest.
Arguments:
- gathers: bfloat16 [4, 96, 96, 256], P('parts', 'xline'), parts along dimension 0, may hold values from -6 to 6
- time_steps: float32 [2], replicated, may hold values from 0.3 to 0.8
- radon_op: bfloat16 [32, 2, 96, 96], P('xline'), may hold values from -0.4375 to 0.4375
Outputs:
- conditioned: bfloat16 [4, 96, 96, 256], P('parts', 'xline'), parts along dimension 0
The draws below stay inside these ranges and needn't reach their ends.
There are 2 independent parts, one for each index of `parts`. The reference program is written for one: setup_inputs(seed, part) draws one part's arguments, and reference() takes and returns one part's arrays. A program takes and returns all parts, laid end to end along the dimension named above; an argument that names none is the same for every part. Nothing has to cross between parts.
All inputs are finite; a program needn't handle non-finite values.
Results may differ from the reference program's by a relative error of at most 0.0072.
Values may be sent and summed in bfloat16 or wider, within the bound.
No kernel may reach another device: no remote copies, remote signals or barrier semaphores. Data moves between devices by JAX's collectives and lax.ppermute only.
A program may use at most 128 MiB of HBM per device.

```python
import math
import jax
import jax.numpy as jnp

IL = 2
NO = 96
NZ = 256
STEPS = 2
XL = 96
NF = 32


def steps_of(own_key, shape, split, smallest, largest):
    gain = 1.0
    for position, parts in split:
        draws = jax.random.uniform(jax.random.fold_in(jax.random.fold_in(own_key, 6), position), (parts,), jnp.float32, smallest / len(split), largest / len(split))
        gain = gain * jnp.repeat(jnp.exp(draws), shape[position] // parts).reshape((-1,) + (1,) * (len(shape) - 1 - position))
    return gain


def centred(rng, extent, spread, bound, cuts=(), kind=jnp.bfloat16):
    values = jax.random.normal(rng, extent, jnp.float32) * spread
    if len(cuts) > 0:
        values = steps_of(rng, extent, cuts, -0.22, 0.18) * values
    return jnp.clip(values, min=-bound, max=bound).astype(kind)


def setup_inputs(seed: int = 0, part: int = 0) -> dict:
    streams_of = jax.random.split(jax.random.key(seed), 4)
    own_keys = jax.random.split(jax.random.fold_in(streams_of[3], part), 4)
    gathers = centred(own_keys[0], (IL, XL, NO, NZ), 1.0, 6.0, ((1, 16),))
    time_steps = jnp.clip(jax.random.uniform(streams_of[1], (STEPS,), jnp.float32, 0.3, 0.8), 0.3, 0.8)
    radon_op = centred(streams_of[2], (NF, 2, NO, NO), (2 * NO) ** -0.5, 0.4375, ((0, 16),))
    return dict(gathers=gathers, time_steps=time_steps, radon_op=radon_op)


def diff_depth(field):
    padded = jnp.pad(field, ((0, 0), (0, 0), (0, 0), (1, 1)))
    return 0.5 * (padded[..., 2:] - padded[..., :-2])


def box_depth(field):
    padded = jnp.pad(field, ((0, 0), (0, 0), (0, 0), (1, 1)))
    return (padded[..., :-2] + padded[..., 1:-1] + padded[..., 2:]) / 3.0


def diff_cross(field):
    return 0.5 * (field[:, 2:] - field[:, :-2])


def box_cross(field):
    return (field[:, :-2] + field[:, 1:-1] + field[:, 2:]) / 3.0


def diffuse(extended, tau_value, columns, total):
    inside = ((columns >= 0) & (columns < total)).astype(jnp.float32)[None, :, None, None]
    grad_cross = diff_cross(extended) * inside[:, 1:-1]
    grad_depth = diff_depth(extended[:, 1:-1]) * inside[:, 1:-1]
    tensor_xx = box_cross(box_depth(grad_cross * grad_cross)) * inside[:, 2:-2]
    tensor_xz = box_cross(box_depth(grad_cross * grad_depth)) * inside[:, 2:-2]
    tensor_zz = box_cross(box_depth(grad_depth * grad_depth)) * inside[:, 2:-2]
    norm_term = 1.0 + tensor_xx + tensor_zz
    inner_x = grad_cross[:, 1:-1]
    inner_z = grad_depth[:, 1:-1]
    flux_cross = inner_x - (tensor_xx * inner_x + tensor_xz * inner_z) / norm_term
    flux_depth = inner_z - (tensor_xz * inner_x + tensor_zz * inner_z) / norm_term
    change = diff_cross(flux_cross) + diff_depth(flux_depth[:, 1:-1])
    return (extended[:, 3:-3] + tau_value * change) * inside[:, 3:-3]


def forward_table(depth, bins):
    zeds = jnp.arange(depth, dtype=jnp.int32)[:, None]
    freqs = jnp.arange(bins, dtype=jnp.int32)[None, :]
    phase = ((zeds * freqs) % depth).astype(jnp.float32) * (2.0 * math.pi / depth)
    return jnp.concatenate([jnp.cos(phase), -jnp.sin(phase)], axis=1).astype(jnp.bfloat16)


def inverse_table(depth, bins):
    freqs = jnp.arange(bins, dtype=jnp.int32)[:, None]
    zeds = jnp.arange(depth, dtype=jnp.int32)[None, :]
    phase = ((zeds * freqs) % depth).astype(jnp.float32) * (2.0 * math.pi / depth)
    weight = jnp.where(freqs == 0, 1.0, 2.0).astype(jnp.float32) / depth
    return jnp.concatenate([weight * jnp.cos(phase), -weight * jnp.sin(phase)], axis=0).astype(jnp.bfloat16)


def reference(gathers, time_steps, radon_op):
    field = gathers.astype(jnp.float32)
    width = field.shape[1]
    columns = jnp.arange(-3, width + 3, dtype=jnp.int32)
    for number in range(STEPS):
        extended = jnp.pad(field, ((0, 0), (3, 3), (0, 0), (0, 0)))
        field = diffuse(extended, time_steps[number], columns, width)
    smooth = field.astype(jnp.bfloat16)
    spectrum = jnp.dot(smooth.reshape(-1, NZ), forward_table(NZ, NF), preferred_element_type=jnp.float32)
    spectrum = spectrum.astype(jnp.bfloat16).reshape(-1, NO, 2, NF)
    real_row = jnp.stack([radon_op[:, 0], -radon_op[:, 1]], axis=1)
    imag_row = jnp.stack([radon_op[:, 1], radon_op[:, 0]], axis=1)
    mats = jnp.stack([real_row, imag_row], axis=1)
    filtered = jnp.einsum("aorf,fqrpo->apqf", spectrum.astype(jnp.float32), mats.astype(jnp.float32))
    filtered = filtered.astype(jnp.bfloat16).reshape(-1, 2 * NF)
    result = jnp.dot(filtered, inverse_table(NZ, NF), preferred_element_type=jnp.float32)
    return result.astype(jnp.bfloat16).reshape(IL, XL, NO, NZ)
```

```python
import functools
import math

import jax
import jax.numpy as jnp
import numpy as np
from jax import lax
from jax.experimental import pallas as pl
from jax.experimental.pallas import tpu as pltpu
from jax.sharding import PartitionSpec as P

F32 = jnp.float32
BF16 = jnp.bfloat16
ROWS = 16


def forward_table(depth, bins):
    phase = (np.arange(depth)[:, None] * np.arange(bins)[None, :] % depth).astype(np.float32)
    phase = phase * np.float32(2.0 * math.pi / depth)
    return np.concatenate([np.cos(phase), -np.sin(phase)], axis=1).astype(BF16)


def inverse_table(depth, bins):
    phase = (np.arange(bins)[:, None] * np.arange(depth)[None, :] % depth).astype(np.float32)
    phase = phase * np.float32(2.0 * math.pi / depth)
    weight = np.where(np.arange(bins)[:, None] == 0, 1.0, 2.0).astype(np.float32) / np.float32(depth)
    return np.concatenate([weight * np.cos(phase), -weight * np.sin(phase)], axis=0).astype(BF16)


def split_matrix(depth):
    half = depth // 2
    source = np.concatenate([2 * np.arange(half), 2 * np.arange(half) + 1])
    return (np.arange(depth)[:, None] == source[None, :]).astype(BF16)


def shifts(half):
    lane = lax.broadcasted_iota(jnp.int32, (ROWS, half), 1)
    first, last = lane == 0, lane == half - 1

    def before(odd):
        return jnp.where(first, 0.0, pltpu.roll(odd, 1, 1))

    def after(even):
        return jnp.where(last, 0.0, pltpu.roll(even, half - 1, 1))

    return before, after


def step_lines(load, store, low, high, quarter, gate, before, after):
    lines = {}

    def line(u):
        if u not in lines:
            lines[u] = load(u)
        return lines[u]

    grads, prods, fluxes, slopes = {}, {}, {}, {}
    for u in range(low - 2, high + 2):
        (ae, ao), (be, bo), (ce, co) = line(u - 1), line(u), line(u + 1)
        gxe, gxo = ce - ae, co - ao
        if u == -1 and gate is not None:
            gxe, gxo = gxe * gate, gxo * gate
        gze, gzo = bo - before(bo), after(be) - be
        grads[u] = gxe, gxo, gze, gzo
        prods[u] = (gxe * gxe, gxo * gxo, gxe * gze, gxo * gzo, gze * gze, gzo * gzo)
        v = u - 1
        if v - 1 in prods:
            sums = [a + b + c for a, b, c in zip(prods[v - 1], prods[v], prods[v + 1])]
            boxes = []
            for even, odd in zip(sums[0::2], sums[1::2]):
                both = even + odd
                boxes.append((both + before(odd), both + after(even)))
            gxe, gxo, gze, gzo = grads[v]
            flux = []
            for part, (gx, gz) in enumerate(((gxe, gze), (gxo, gzo))):
                sxx, sxz, szz = (box[part] for box in boxes)
                top = szz + 36.0
                inverse = 1.0 / (top + sxx)
                flux.append(((top * gx - sxz * gz) * inverse, ((sxx + 36.0) * gz - sxz * gx) * inverse))
            (fxe, fze), (fxo, fzo) = flux
            fluxes[v] = fxe, fxo
            slopes[v] = fzo - before(fzo), after(fze) - fze
        w = v - 1
        if low <= w < high:
            (fe, fo), (le, lo), (re, ro), (se, so) = line(w), fluxes[w - 1], fluxes[w + 1], slopes[w]
            fe = fe + quarter * ((re - le) + se)
            fo = fo + quarter * ((ro - lo) + so)
            if w == -1:
                fe, fo = fe * gate, fo * gate
            store(w, fe, fo)


def place_of(flip, lines):
    def place(u):
        if u < 0:
            return 0, jnp.where(flip, -1 - u, lines + u)
        if u < lines:
            return 1, jnp.where(flip, lines - 1 - u, u)
        return 2, jnp.where(flip, 2 * lines - 1 - u, u - lines)

    return place


def strips(offsets, body):
    def run(s, carry):
        body(pl.ds(pl.multiple_of(s * ROWS, ROWS), ROWS))
        return carry

    lax.fori_loop(0, offsets // ROWS, run, 0)


def split_block(block, split):
    lines, offsets, depth = block.shape
    plain = jnp.dot(block.reshape(lines * offsets, depth), split, preferred_element_type=F32)
    return plain.reshape(lines, offsets, depth)


def early_kernel(tau_ref, own_ref, mate_ref, split_ref, out_ref, field_ref):
    _, lines, offsets, depth = own_ref.shape
    share = out_ref.shape[0]
    half = depth // 2
    parity = lax.axis_index("xline") % 2
    place = place_of(parity == 1, lines)
    places = {u: place(u) for u in range(2 * lines)}
    for i in range(share):
        at = parity * share + i
        field_ref[0] = split_block(own_ref[at], split_ref[...])
        field_ref[1] = split_block(mate_ref[at], split_ref[...])

        def strip(rows, i=i):
            before, after = shifts(half)

            def load(u):
                b, spot = places[u]
                return field_ref[b - 1, spot, rows, :half], field_ref[b - 1, spot, rows, half:]

            def store(u, even, odd):
                out_ref[i, u - 3, rows, :half] = even
                out_ref[i, u - 3, rows, half:] = odd

            step_lines(load, store, 3, lines + 3, tau_ref[0] * 0.25, None, before, after)

        strips(offsets, strip)


def late_kernel(inline, start, tau_ref, halo_hbm, own_hbm, first_hbm, other_hbm, split_ref, table_ref, out_ref, halo_ref, own_ref, first_ref, field_ref, mid_ref, smooth_ref, sems):
    lines, offsets, depth = own_ref.shape
    half = depth // 2
    share = first_hbm.shape[0]
    me = lax.axis_index("xline")
    last = lax.axis_size("xline") - 1
    parity = me % 2
    gate = jnp.where((me == 0) | (me == last), 0.0, 1.0)
    mine = parity == inline // share
    place = place_of(parity == 1, lines)
    places = {u: place(u) for u in range(-lines, lines)}
    some = pl.ds(start, offsets)
    halo_copy = pltpu.make_async_copy(halo_hbm.at[0, :, some], halo_ref, sems.at[0])
    own_copy = pltpu.make_async_copy(own_hbm.at[inline, :, some], own_ref, sems.at[1])
    first_copy = pltpu.make_async_copy(first_hbm.at[inline % share, :, some], first_ref, sems.at[2])
    other_copy = pltpu.make_async_copy(other_hbm.at[inline % share, :, some], first_ref, sems.at[2])
    own_copy.start()
    halo_copy.start()
    pl.when(mine)(lambda: first_copy.start())
    pl.when(jnp.logical_not(mine))(lambda: other_copy.start())
    own_copy.wait()
    field_ref[1] = split_block(own_ref[...], split_ref[...])
    halo_copy.wait()
    field_ref[0] = split_block(halo_ref[...], split_ref[...])
    first_copy.wait()

    def strip(rows):
        before, after = shifts(half)

        def load(u):
            b, spot = places[u]
            return field_ref[b, spot, rows, :half], field_ref[b, spot, rows, half:]

        def keep(u, even, odd):
            mid_ref[u + 3, :, :half] = even
            mid_ref[u + 3, :, half:] = odd

        def fetch(u):
            if u < 3:
                return mid_ref[u + 3, :, :half], mid_ref[u + 3, :, half:]
            spot = jnp.where(mine, u - 3, lines + 2 - u)
            return first_ref[spot, rows, :half], first_ref[spot, rows, half:]

        def store(u, even, odd):
            spot = places[u][1]
            smooth_ref[spot, rows, :half] = even
            smooth_ref[spot, rows, half:] = odd

        step_lines(load, keep, -3, 3, tau_ref[0] * 0.25, gate, before, after)
        step_lines(fetch, store, 0, lines, tau_ref[1] * 0.25, gate, before, after)

    strips(offsets, strip)
    for x in range(lines):
        smooth = smooth_ref[x].astype(BF16)
        spectrum = lax.dot_general(table_ref[...], smooth, (((1,), (1,)), ((), ())), preferred_element_type=F32)
        out_ref[x] = spectrum.astype(BF16)


def radon_kernel(near, apart, *refs):
    *spec_refs, mine_ref, theirs_ref, mine_mate_ref, theirs_mate_ref, inverse_ref, out_ref, bins_ref, done_ref = refs
    lines, twice, _ = spec_refs[0].shape
    bins = twice // 2
    rows = bins_ref.shape[0] // twice
    me = lax.axis_index("xline")
    for i, spec_ref in enumerate(spec_refs):
        for x in range(lines):
            at = (i * lines + x) * twice
            bins_ref[at : at + twice, :] = spec_ref[x].astype(F32)
    held = mine_ref.shape[1]
    for ref, extra in ((mine_ref, 0), (mine_mate_ref, 1), (theirs_ref, apart), (theirs_mate_ref, 1 ^ apart)):
        for j, offset in enumerate(near):
            owner = me ^ (offset ^ extra)
            for b in range(held):
                k = owner * held + b
                real = bins_ref[pl.ds(k, rows, stride=twice), :]
                imag = bins_ref[pl.ds(bins + k, rows, stride=twice), :]
                both = jnp.concatenate([real, imag], axis=0).astype(BF16)
                by_real = lax.dot_general(both, ref[j, b, 0], (((1,), (1,)), ((), ())), preferred_element_type=F32)
                by_imag = lax.dot_general(both, ref[j, b, 1], (((1,), (1,)), ((), ())), preferred_element_type=F32)
                done_ref[pl.ds(k, rows, stride=twice), :] = by_real[:rows] - by_imag[rows:]
                done_ref[pl.ds(bins + k, rows, stride=twice), :] = by_imag[:rows] + by_real[rows:]
    for i in range(len(spec_refs)):
        for x in range(lines):
            at = (i * lines + x) * twice
            filtered = done_ref[at : at + twice, :].astype(BF16)
            result = lax.dot_general(filtered, inverse_ref[...], (((0,), (0,)), ((), ())), preferred_element_type=F32)
            out_ref[i, x] = result.astype(BF16)


def swapped(gathers, time_steps, radon_op):
    inlines, lines, offsets, depth = gathers.shape
    devices = lax.axis_size("xline")
    held = radon_op.shape[0]
    bins = held * devices
    apart = 4
    near = tuple(o for o in range(0, devices, 2) if not o & apart)

    def swap(value, mask):
        return lax.ppermute(value, "xline", [(i, i ^ mask) for i in range(devices)])

    cross = [(i, i + 1) for i in range(1, devices - 1, 2)] + [(i + 1, i) for i in range(1, devices - 1, 2)]
    pieces = [radon_op]
    for o in reversed(near[1:]):
        pieces.append(swap(radon_op, o))
    pieces = [pieces[0]] + pieces[:0:-1]
    mate = swap(gathers, 1)
    halos = []
    for i in range(inlines):
        halos.append(lax.ppermute(gathers[i : i + 1], "xline", cross))
    mine = jnp.stack(pieces)
    theirs = swap(mine, apart)
    mine_mate = swap(mine, 1)
    theirs_mate = swap(theirs, 1)

    vmem = pl.BlockSpec(memory_space=pltpu.VMEM)
    smem = pl.BlockSpec(memory_space=pltpu.SMEM)
    table = forward_table(depth, bins)
    table = np.concatenate([table[0::2], table[1::2]], axis=0).T
    split = jnp.asarray(split_matrix(depth))
    any_space = pl.BlockSpec(memory_space=pltpu.HBM)
    share = inlines // 2
    first = pl.pallas_call(
        early_kernel,
        out_shape=jax.ShapeDtypeStruct((share, lines, offsets, depth), F32),
        in_specs=[smem] + [vmem] * 3,
        out_specs=vmem,
        scratch_shapes=[pltpu.VMEM((2, lines, offsets, depth), F32)],
        cost_estimate=pl.CostEstimate(flops=3_000_000_000, bytes_accessed=0, transcendentals=0),
        name="early",
    )(time_steps, gathers, mate, split)
    other = swap(first, 1)
    spectra = []
    half = offsets
    starts = (0,)
    for i in range(inlines):
        for start in starts:
            spectra.append(
                pl.pallas_call(
                    functools.partial(late_kernel, i, start),
                    out_shape=jax.ShapeDtypeStruct((lines, 2 * bins, half), BF16),
                    in_specs=[smem] + [any_space] * 4 + [vmem] * 2,
                    out_specs=vmem,
                    scratch_shapes=[
                        pltpu.VMEM((lines, half, depth), BF16),
                        pltpu.VMEM((lines, half, depth), BF16),
                        pltpu.VMEM((lines, half, depth), F32),
                        pltpu.VMEM((2, lines, half, depth), F32),
                        pltpu.VMEM((6, ROWS, depth), F32),
                        pltpu.VMEM((lines, half, depth), F32),
                        pltpu.SemaphoreType.DMA((3,)),
                    ],
                    cost_estimate=pl.CostEstimate(flops=3_000_000_000, bytes_accessed=0, transcendentals=0),
                )(time_steps, halos[i], gathers, first, other, split, jnp.asarray(table))
            )
    rows = -(-inlines * lines // 16) * 16
    return pl.pallas_call(
        functools.partial(radon_kernel, near, apart),
        out_shape=jax.ShapeDtypeStruct((inlines, lines, offsets, depth), BF16),
        in_specs=[vmem] * (len(spectra) + 5),
        out_specs=vmem,
        scratch_shapes=[
            pltpu.VMEM((rows * 2 * bins, offsets), F32),
            pltpu.VMEM((rows * 2 * bins, offsets), F32),
        ],
        cost_estimate=pl.CostEstimate(flops=int(4e-6 * 1.0e15), bytes_accessed=0, transcendentals=0),
        name="radon",
    )(*spectra, mine, theirs, mine_mate, theirs_mate, jnp.asarray(inverse_table(depth, bins)))


def solution(mesh):
    return jax.shard_map(
        swapped,
        mesh=mesh,
        in_specs=(P("parts", "xline", None, None), P(), P("xline", None, None, None)),
        out_specs=P("parts", "xline", None, None),
        check_vma=False,
    )
```

```python
import functools
import math

import jax
import jax.numpy as jnp
import numpy as np
from jax import lax
from jax.experimental import pallas as pl
from jax.experimental.pallas import tpu as pltpu
from jax.sharding import PartitionSpec as P

F32 = jnp.float32
BF16 = jnp.bfloat16
ROWS = 16


def forward_table(depth, bins):
    phase = (np.arange(depth)[:, None] * np.arange(bins)[None, :] % depth).astype(np.float32)
    phase = phase * np.float32(2.0 * math.pi / depth)
    return np.concatenate([np.cos(phase), -np.sin(phase)], axis=1).astype(BF16)


def inverse_table(depth, bins):
    phase = (np.arange(bins)[:, None] * np.arange(depth)[None, :] % depth).astype(np.float32)
    phase = phase * np.float32(2.0 * math.pi / depth)
    weight = np.where(np.arange(bins)[:, None] == 0, 1.0, 2.0).astype(np.float32) / np.float32(depth)
    return np.concatenate([weight * np.cos(phase), -weight * np.sin(phase)], axis=0).astype(BF16)


def split_matrix(depth):
    half = depth // 2
    source = np.concatenate([2 * np.arange(half), 2 * np.arange(half) + 1])
    return (np.arange(depth)[:, None] == source[None, :]).astype(BF16)


def shifts(half):
    lane = lax.broadcasted_iota(jnp.int32, (ROWS, half), 1)
    first, last = lane == 0, lane == half - 1

    def before(odd):
        return jnp.where(first, 0.0, pltpu.roll(odd, 1, 1))

    def after(even):
        return jnp.where(last, 0.0, pltpu.roll(even, half - 1, 1))

    return before, after


def step_lines(load, store, low, high, quarter, gate, before, after):
    lines = {}

    def line(u):
        if u not in lines:
            lines[u] = load(u)
        return lines[u]

    grads, prods, fluxes, slopes = {}, {}, {}, {}
    for u in range(low - 2, high + 2):
        (ae, ao), (be, bo), (ce, co) = line(u - 1), line(u), line(u + 1)
        gxe, gxo = ce - ae, co - ao
        if u == -1 and gate is not None:
            gxe, gxo = gxe * gate, gxo * gate
        gze, gzo = bo - before(bo), after(be) - be
        grads[u] = gxe, gxo, gze, gzo
        prods[u] = (gxe * gxe, gxo * gxo, gxe * gze, gxo * gzo, gze * gze, gzo * gzo)
        v = u - 1
        if v - 1 in prods:
            sums = [a + b + c for a, b, c in zip(prods[v - 1], prods[v], prods[v + 1])]
            boxes = []
            for even, odd in zip(sums[0::2], sums[1::2]):
                both = even + odd
                boxes.append((both + before(odd), both + after(even)))
            gxe, gxo, gze, gzo = grads[v]
            flux = []
            for part, (gx, gz) in enumerate(((gxe, gze), (gxo, gzo))):
                sxx, sxz, szz = (box[part] for box in boxes)
                top = szz + 36.0
                inverse = 1.0 / (top + sxx)
                flux.append(((top * gx - sxz * gz) * inverse, ((sxx + 36.0) * gz - sxz * gx) * inverse))
            (fxe, fze), (fxo, fzo) = flux
            fluxes[v] = fxe, fxo
            slopes[v] = fzo - before(fzo), after(fze) - fze
        w = v - 1
        if low <= w < high:
            (fe, fo), (le, lo), (re, ro), (se, so) = line(w), fluxes[w - 1], fluxes[w + 1], slopes[w]
            fe = fe + quarter * ((re - le) + se)
            fo = fo + quarter * ((ro - lo) + so)
            if w == -1:
                fe, fo = fe * gate, fo * gate
            store(w, fe, fo)


def place_of(flip, lines):
    def place(u):
        if u < 0:
            return 0, jnp.where(flip, -1 - u, lines + u)
        if u < lines:
            return 1, jnp.where(flip, lines - 1 - u, u)
        return 2, jnp.where(flip, 2 * lines - 1 - u, u - lines)

    return place


def strips(offsets, body):
    def run(s, carry):
        body(pl.ds(pl.multiple_of(s * ROWS, ROWS), ROWS))
        return carry

    lax.fori_loop(0, offsets // ROWS, run, 0)


def split_block(block, split):
    lines, offsets, depth = block.shape
    plain = jnp.dot(block.reshape(lines * offsets, depth), split, preferred_element_type=F32)
    return plain.reshape(lines, offsets, depth)


def early_kernel(tau_ref, own_ref, mate_ref, split_ref, out_ref, field_ref):
    _, lines, offsets, depth = own_ref.shape
    share = out_ref.shape[0]
    half = depth // 2
    parity = lax.axis_index("xline") % 2
    place = place_of(parity == 1, lines)
    places = {u: place(u) for u in range(2 * lines)}
    for i in range(share):
        at = parity * share + i
        field_ref[0] = split_block(own_ref[at], split_ref[...])
        field_ref[1] = split_block(mate_ref[at], split_ref[...])

        def strip(rows, i=i):
            before, after = shifts(half)

            def load(u):
                b, spot = places[u]
                return field_ref[b - 1, spot, rows, :half], field_ref[b - 1, spot, rows, half:]

            def store(u, even, odd):
                out_ref[i, u - 3, rows, :half] = even
                out_ref[i, u - 3, rows, half:] = odd

            step_lines(load, store, 3, lines + 3, tau_ref[0] * 0.25, None, before, after)

        strips(offsets, strip)


def late_kernel(inline, start, tau_ref, halo_hbm, own_hbm, first_hbm, other_hbm, split_ref, table_ref, out_ref, halo_ref, own_ref, first_ref, field_ref, mid_ref, smooth_ref, sems):
    lines, offsets, depth = own_ref.shape
    half = depth // 2
    share = first_hbm.shape[0]
    me = lax.axis_index("xline")
    last = lax.axis_size("xline") - 1
    parity = me % 2
    gate = jnp.where((me == 0) | (me == last), 0.0, 1.0)
    mine = parity == inline // share
    place = place_of(parity == 1, lines)
    places = {u: place(u) for u in range(-lines, lines)}
    some = pl.ds(start, offsets)
    halo_copy = pltpu.make_async_copy(halo_hbm.at[0, :, some], halo_ref, sems.at[0])
    own_copy = pltpu.make_async_copy(own_hbm.at[inline, :, some], own_ref, sems.at[1])
    first_copy = pltpu.make_async_copy(first_hbm.at[inline % share, :, some], first_ref, sems.at[2])
    other_copy = pltpu.make_async_copy(other_hbm.at[inline % share, :, some], first_ref, sems.at[2])
    own_copy.start()
    halo_copy.start()
    pl.when(mine)(lambda: first_copy.start())
    pl.when(jnp.logical_not(mine))(lambda: other_copy.start())
    own_copy.wait()
    field_ref[1] = split_block(own_ref[...], split_ref[...])
    halo_copy.wait()
    field_ref[0] = split_block(halo_ref[...], split_ref[...])
    first_copy.wait()

    def strip(rows):
        before, after = shifts(half)

        def load(u):
            b, spot = places[u]
            return field_ref[b, spot, rows, :half], field_ref[b, spot, rows, half:]

        def keep(u, even, odd):
            mid_ref[u + 3, :, :half] = even
            mid_ref[u + 3, :, half:] = odd

        def fetch(u):
            if u < 3:
                return mid_ref[u + 3, :, :half], mid_ref[u + 3, :, half:]
            spot = jnp.where(mine, u - 3, lines + 2 - u)
            return first_ref[spot, rows, :half], first_ref[spot, rows, half:]

        def store(u, even, odd):
            spot = places[u][1]
            smooth_ref[spot, rows, :half] = even
            smooth_ref[spot, rows, half:] = odd

        step_lines(load, keep, -3, 3, tau_ref[0] * 0.25, gate, before, after)
        step_lines(fetch, store, 0, lines, tau_ref[1] * 0.25, gate, before, after)

    strips(offsets, strip)
    for x in range(lines):
        smooth = smooth_ref[x].astype(BF16)
        spectrum = lax.dot_general(table_ref[...], smooth, (((1,), (1,)), ((), ())), preferred_element_type=F32)
        out_ref[x] = spectrum.astype(BF16)


def radon_kernel(near, apart, *refs):
    *spec_refs, mine_ref, theirs_ref, mine_mate_ref, theirs_mate_ref, inverse_ref, out_ref, bins_ref, done_ref = refs
    lines, twice, _ = spec_refs[0].shape
    bins = twice // 2
    rows = bins_ref.shape[0] // twice
    me = lax.axis_index("xline")
    for i, spec_ref in enumerate(spec_refs):
        for x in range(lines):
            at = (i * lines + x) * twice
            bins_ref[at : at + twice, :] = spec_ref[x].astype(F32)
    held = mine_ref.shape[1]
    for ref, extra in ((mine_ref, 0), (mine_mate_ref, 1), (theirs_ref, apart), (theirs_mate_ref, 1 ^ apart)):
        for j, offset in enumerate(near):
            owner = me ^ (offset ^ extra)
            for b in range(held):
                k = owner * held + b
                real = bins_ref[pl.ds(k, rows, stride=twice), :]
                imag = bins_ref[pl.ds(bins + k, rows, stride=twice), :]
                both = jnp.concatenate([real, imag], axis=0).astype(BF16)
                by_real = lax.dot_general(both, ref[j, b, 0], (((1,), (1,)), ((), ())), preferred_element_type=F32)
                by_imag = lax.dot_general(both, ref[j, b, 1], (((1,), (1,)), ((), ())), preferred_element_type=F32)
                done_ref[pl.ds(k, rows, stride=twice), :] = by_real[:rows] - by_imag[rows:]
                done_ref[pl.ds(bins + k, rows, stride=twice), :] = by_imag[:rows] + by_real[rows:]
    for i in range(len(spec_refs)):
        for x in range(lines):
            at = (i * lines + x) * twice
            filtered = done_ref[at : at + twice, :].astype(BF16)
            result = lax.dot_general(filtered, inverse_ref[...], (((0,), (0,)), ((), ())), preferred_element_type=F32)
            out_ref[i, x] = result.astype(BF16)


def swapped(gathers, time_steps, radon_op):
    inlines, lines, offsets, depth = gathers.shape
    devices = lax.axis_size("xline")
    held = radon_op.shape[0]
    bins = held * devices
    apart = 4
    near = tuple(o for o in range(0, devices, 2) if not o & apart)

    def swap(value, mask):
        return lax.ppermute(value, "xline", [(i, i ^ mask) for i in range(devices)])

    cross = [(i, i + 1) for i in range(1, devices - 1, 2)] + [(i + 1, i) for i in range(1, devices - 1, 2)]
    pieces = [radon_op]
    for o in reversed(near[1:]):
        pieces.append(swap(radon_op, o))
    pieces = [pieces[0]] + pieces[:0:-1]
    mate = swap(gathers, 1)
    halos = []
    for i in range(inlines):
        halos.append(lax.ppermute(gathers[i : i + 1], "xline", cross))
    mine = jnp.stack(pieces)
    theirs = swap(mine, apart)
    mine_mate = swap(mine, 1)
    theirs_mate = swap(theirs, 1)

    vmem = pl.BlockSpec(memory_space=pltpu.VMEM)
    smem = pl.BlockSpec(memory_space=pltpu.SMEM)
    table = forward_table(depth, bins)
    table = np.concatenate([table[0::2], table[1::2]], axis=0).T
    split = jnp.asarray(split_matrix(depth))
    any_space = pl.BlockSpec(memory_space=pl.ANY)
    share = inlines // 2
    first = pl.pallas_call(
        early_kernel,
        out_shape=jax.ShapeDtypeStruct((share, lines, offsets, depth), F32),
        in_specs=[smem] + [vmem] * 3,
        out_specs=vmem,
        scratch_shapes=[pltpu.VMEM((2, lines, offsets, depth), F32)],
        cost_estimate=pl.CostEstimate(flops=3_000_000_000, bytes_accessed=0, transcendentals=0),
        compiler_params=pltpu.CompilerParams(vmem_limit_bytes=16 << 20),
        name="early",
    )(time_steps, gathers, mate, split)
    other = swap(first, 1)
    spectra = []
    half = offsets
    starts = (0,)
    for i in range(inlines):
        for start in starts:
            spectra.append(
                pl.pallas_call(
                    functools.partial(late_kernel, i, start),
                    out_shape=jax.ShapeDtypeStruct((lines, 2 * bins, half), BF16),
                    in_specs=[smem] + [any_space] * 4 + [vmem] * 2,
                    out_specs=vmem,
                    scratch_shapes=[
                        pltpu.VMEM((lines, half, depth), BF16),
                        pltpu.VMEM((lines, half, depth), BF16),
                        pltpu.VMEM((lines, half, depth), F32),
                        pltpu.VMEM((2, lines, half, depth), F32),
                        pltpu.VMEM((6, ROWS, depth), F32),
                        pltpu.VMEM((lines, half, depth), F32),
                        pltpu.SemaphoreType.DMA((3,)),
                    ],
                    cost_estimate=pl.CostEstimate(flops=3_000_000_000, bytes_accessed=0, transcendentals=0),
                    compiler_params=pltpu.CompilerParams(vmem_limit_bytes=16 << 20),
                )(time_steps, halos[i], gathers, first, other, split, jnp.asarray(table))
            )
    rows = -(-inlines * lines // 16) * 16
    return pl.pallas_call(
        functools.partial(radon_kernel, near, apart),
        out_shape=jax.ShapeDtypeStruct((inlines, lines, offsets, depth), BF16),
        in_specs=[vmem] * (len(spectra) + 5),
        out_specs=vmem,
        scratch_shapes=[
            pltpu.VMEM((rows * 2 * bins, offsets), F32),
            pltpu.VMEM((rows * 2 * bins, offsets), F32),
        ],
        cost_estimate=pl.CostEstimate(flops=int(4e-6 * 1.0e15), bytes_accessed=0, transcendentals=0),
        compiler_params=pltpu.CompilerParams(vmem_limit_bytes=16 << 20),
        name="radon",
    )(*spectra, mine, theirs, mine_mate, theirs_mate, jnp.asarray(inverse_table(depth, bins)))


def solution(mesh):
    return jax.shard_map(
        swapped,
        mesh=mesh,
        in_specs=(P("parts", "xline", None, None), P(), P("xline", None, None, None)),
        out_specs=P("parts", "xline", None, None),
        check_vma=False,
    )
```

```python
import functools
import math

import jax
import jax.numpy as jnp
import numpy as np
from jax import lax
from jax.experimental import pallas as pl
from jax.experimental.pallas import tpu as pltpu
from jax.sharding import PartitionSpec as P

F32 = jnp.float32
BF16 = jnp.bfloat16
ROWS = 32


def forward_table(depth, bins):
    phase = (np.arange(depth)[:, None] * np.arange(bins)[None, :] % depth).astype(np.float32)
    phase = phase * np.float32(2.0 * math.pi / depth)
    return np.concatenate([np.cos(phase), -np.sin(phase)], axis=1).astype(BF16)


def inverse_table(depth, bins):
    phase = (np.arange(bins)[:, None] * np.arange(depth)[None, :] % depth).astype(np.float32)
    phase = phase * np.float32(2.0 * math.pi / depth)
    weight = np.where(np.arange(bins)[:, None] == 0, 1.0, 2.0).astype(np.float32) / np.float32(depth)
    return np.concatenate([weight * np.cos(phase), -weight * np.sin(phase)], axis=0).astype(BF16)


def split_matrix(depth):
    half = depth // 2
    source = np.concatenate([2 * np.arange(half), 2 * np.arange(half) + 1])
    return (np.arange(depth)[:, None] == source[None, :]).astype(BF16)


def shifts(half):
    lane = lax.broadcasted_iota(jnp.int32, (ROWS, half), 1)
    first, last = lane == 0, lane == half - 1
    zero = jnp.zeros((ROWS, half), BF16)

    def before(odd):
        return jnp.where(first, zero, pltpu.roll(odd, 1, 1))

    def after(even):
        return jnp.where(last, zero, pltpu.roll(even, half - 1, 1))

    return before, after


def step_lines(load, store, low, high, quarter, gate, before, after):
    narrow = {}

    def line(u):
        if u not in narrow:
            narrow[u] = tuple(part.astype(BF16) for part in load(u))
        return narrow[u]

    grads, prods, fluxes, slopes = {}, {}, {}, {}
    for u in range(low - 2, high + 2):
        (ae, ao), (be, bo), (ce, co) = line(u - 1), line(u), line(u + 1)
        gxe, gxo = ce - ae, co - ao
        if u == -1 and gate is not None:
            gxe, gxo = gxe * gate.astype(BF16), gxo * gate.astype(BF16)
        gze, gzo = bo - before(bo), after(be) - be
        grads[u] = gxe, gxo, gze, gzo
        prods[u] = (gxe * gxe, gxo * gxo, gxe * gze, gxo * gzo, gze * gze, gzo * gzo)
        v = u - 1
        if v - 1 in prods:
            sums = [a + b + c for a, b, c in zip(prods[v - 1], prods[v], prods[v + 1])]
            boxes = []
            for even, odd in zip(sums[0::2], sums[1::2]):
                both = even + odd
                boxes.append((both + before(odd), both + after(even)))
            gxe, gxo, gze, gzo = grads[v]
            flux = []
            for part, (gx, gz) in enumerate(((gxe, gze), (gxo, gzo))):
                sxx, sxz, szz = (box[part] for box in boxes)
                inverse = (1.0 / ((sxx + szz).astype(F32) + 36.0)).astype(BF16)
                flux.append((gx - (sxx * gx + sxz * gz) * inverse, gz - (sxz * gx + szz * gz) * inverse))
            (fxe, fze), (fxo, fzo) = flux
            fluxes[v] = fxe.astype(F32), fxo.astype(F32)
            slopes[v] = fzo.astype(F32) - before(fzo).astype(F32), after(fze).astype(F32) - fze.astype(F32)
        w = v - 1
        if low <= w < high:
            (fe, fo), (le, lo), (re, ro), (se, so) = load(w), fluxes[w - 1], fluxes[w + 1], slopes[w]
            fe = fe + quarter * ((re - le) + se)
            fo = fo + quarter * ((ro - lo) + so)
            if w == -1 and gate is not None:
                fe, fo = fe * gate, fo * gate
            store(w, fe, fo)


def place_of(flip, lines):
    def place(u):
        if u < 0:
            return 0, jnp.where(flip, -1 - u, lines + u)
        if u < lines:
            return 1, jnp.where(flip, lines - 1 - u, u)
        return 2, jnp.where(flip, 2 * lines - 1 - u, u - lines)

    return place


def strips(offsets, body):
    def run(s, carry):
        body(pl.ds(pl.multiple_of(s * ROWS, ROWS), ROWS))
        return carry

    lax.fori_loop(0, offsets // ROWS, run, 0)


def split_block(block, split):
    lines, offsets, depth = block.shape
    plain = jnp.dot(block.reshape(lines * offsets, depth), split, preferred_element_type=F32)
    return plain.reshape(lines, offsets, depth)


def inline_at(parity, turn, share):
    return jnp.where(parity == 1, (share + turn) % (2 * share), turn)


def early_kernel(tau_ref, own_ref, mate_ref, split_ref, out_ref, field_ref):
    _, lines, offsets, depth = own_ref.shape
    share = out_ref.shape[0]
    half = depth // 2
    parity = lax.axis_index("xline") % 2
    place = place_of(parity == 1, lines)
    places = {u: place(u) for u in range(2 * lines)}
    for i in range(share):
        at = parity * share + i
        field_ref[0] = split_block(own_ref[at], split_ref[...])
        field_ref[1] = split_block(mate_ref[at], split_ref[...])

        def strip(rows, i=i):
            before, after = shifts(half)

            def load(u):
                b, spot = places[u]
                return field_ref[b - 1, spot, rows, :half], field_ref[b - 1, spot, rows, half:]

            def store(u, even, odd):
                out_ref[i, u - 3, rows, :half] = even
                out_ref[i, u - 3, rows, half:] = odd

            step_lines(load, store, 3, lines + 3, tau_ref[0] * 0.25, None, before, after)

        strips(offsets, strip)


def late_kernel(turn, tau_ref, halo_hbm, own_hbm, first_hbm, split_ref, table_ref, out_ref, halo_ref, own_ref, first_ref, field_ref, mid_ref, smooth_ref, sems):
    lines, offsets, depth = own_ref.shape
    half = depth // 2
    share = first_hbm.shape[0]
    me = lax.axis_index("xline")
    last = lax.axis_size("xline") - 1
    parity = me % 2
    gate = jnp.where((me == 0) | (me == last), 0.0, 1.0)
    mine = turn < share
    place = place_of(parity == 1, lines)
    places = {u: place(u) for u in range(-lines, lines)}
    inline = inline_at(parity, turn, share)
    halo_copy = pltpu.make_async_copy(halo_hbm.at[0], halo_ref, sems.at[0])
    own_copy = pltpu.make_async_copy(own_hbm.at[inline], own_ref, sems.at[1])
    first_copy = pltpu.make_async_copy(first_hbm.at[turn % share], first_ref, sems.at[2])
    own_copy.start()
    halo_copy.start()
    first_copy.start()
    own_copy.wait()
    field_ref[1] = split_block(own_ref[...], split_ref[...])
    halo_copy.wait()
    field_ref[0] = split_block(halo_ref[...], split_ref[...])
    first_copy.wait()

    def strip(rows):
        before, after = shifts(half)

        def load(u):
            b, spot = places[u]
            return field_ref[b, spot, rows, :half], field_ref[b, spot, rows, half:]

        def keep(u, even, odd):
            mid_ref[u + 3, :, :half] = even
            mid_ref[u + 3, :, half:] = odd

        def fetch(u):
            if u < 3:
                return mid_ref[u + 3, :, :half], mid_ref[u + 3, :, half:]
            spot = u - 3 if mine else lines + 2 - u
            return first_ref[spot, rows, :half], first_ref[spot, rows, half:]

        def store(u, even, odd):
            spot = places[u][1]
            smooth_ref[spot, rows, :half] = even
            smooth_ref[spot, rows, half:] = odd

        step_lines(load, keep, -3, 3, tau_ref[0] * 0.25, gate, before, after)
        step_lines(fetch, store, 0, lines, tau_ref[1] * 0.25, gate, before, after)

    strips(offsets, strip)
    for x in range(lines):
        smooth = smooth_ref[x].astype(BF16)
        spectrum = lax.dot_general(table_ref[...], smooth, (((1,), (1,)), ((), ())), preferred_element_type=F32)
        out_ref[x] = spectrum.astype(BF16)


def radon_kernel(near, apart, *refs):
    *spec_refs, mine_ref, theirs_ref, mine_mate_ref, theirs_mate_ref, inverse_ref, out_ref, bins_ref, done_ref = refs
    lines, twice, _ = spec_refs[0].shape
    bins = twice // 2
    rows = bins_ref.shape[0] // twice
    me = lax.axis_index("xline")
    for i, spec_ref in enumerate(spec_refs):
        for x in range(lines):
            at = (i * lines + x) * twice
            bins_ref[at : at + twice, :] = spec_ref[x].astype(F32)
    held = mine_ref.shape[1]
    for ref, extra in ((mine_ref, 0), (mine_mate_ref, 1), (theirs_ref, apart), (theirs_mate_ref, 1 ^ apart)):
        for j, offset in enumerate(near):
            owner = me ^ (offset ^ extra)
            for b in range(held):
                k = owner * held + b
                real = bins_ref[pl.ds(k, rows, stride=twice), :]
                imag = bins_ref[pl.ds(bins + k, rows, stride=twice), :]
                both = jnp.concatenate([real, imag], axis=0).astype(BF16)
                by_real = lax.dot_general(both, ref[j, b, 0], (((1,), (1,)), ((), ())), preferred_element_type=F32)
                by_imag = lax.dot_general(both, ref[j, b, 1], (((1,), (1,)), ((), ())), preferred_element_type=F32)
                done_ref[pl.ds(k, rows, stride=twice), :] = by_real[:rows] - by_imag[rows:]
                done_ref[pl.ds(bins + k, rows, stride=twice), :] = by_imag[:rows] + by_real[rows:]
    for i in range(len(spec_refs)):
        inline = inline_at(me % 2, i, len(spec_refs) // 2)
        for x in range(lines):
            at = (i * lines + x) * twice
            filtered = done_ref[at : at + twice, :].astype(BF16)
            result = lax.dot_general(filtered, inverse_ref[...], (((0,), (0,)), ((), ())), preferred_element_type=F32)
            out_ref[inline, x] = result.astype(BF16)


def swapped(gathers, time_steps, radon_op):
    inlines, lines, offsets, depth = gathers.shape
    devices = lax.axis_size("xline")
    held = radon_op.shape[0]
    bins = held * devices
    apart = 4
    near = tuple(o for o in range(0, devices, 2) if not o & apart)

    def swap(value, mask):
        return lax.ppermute(value, "xline", [(i, i ^ mask) for i in range(devices)])

    cross = [(i, i + 1) for i in range(1, devices - 1, 2)] + [(i + 1, i) for i in range(1, devices - 1, 2)]
    pieces = [radon_op]
    for o in reversed(near[1:]):
        pieces.append(swap(radon_op, o))
    pieces = [pieces[0]] + pieces[:0:-1]
    mate = swap(gathers, 1)
    halos = []
    for i in range(inlines):
        at = inline_at(1 - lax.axis_index("xline") % 2, i, inlines // 2)
        sent = lax.dynamic_slice_in_dim(gathers, at, 1, axis=0)
        halos.append(lax.ppermute(sent, "xline", cross))
    mine = jnp.stack(pieces)
    theirs = swap(mine, apart)
    mine_mate = swap(mine, 1)
    theirs_mate = swap(theirs, 1)

    vmem = pl.BlockSpec(memory_space=pltpu.VMEM)
    smem = pl.BlockSpec(memory_space=pltpu.SMEM)
    table = forward_table(depth, bins)
    table = np.concatenate([table[0::2], table[1::2]], axis=0).T
    split = jnp.asarray(split_matrix(depth))
    any_space = pl.BlockSpec(memory_space=pl.ANY)
    share = inlines // 2
    first = pl.pallas_call(
        early_kernel,
        out_shape=jax.ShapeDtypeStruct((share, lines, offsets, depth), F32),
        in_specs=[smem] + [vmem] * 3,
        out_specs=vmem,
        scratch_shapes=[pltpu.VMEM((2, lines, offsets, depth), F32)],
        cost_estimate=pl.CostEstimate(flops=3_000_000_000, bytes_accessed=0, transcendentals=0),
        compiler_params=pltpu.CompilerParams(vmem_limit_bytes=16 << 20),
        name="early",
    )(time_steps, gathers, mate, split)
    other = swap(first, 1)
    spectra = []
    for i in range(inlines):
        spectra.append(
            pl.pallas_call(
                functools.partial(late_kernel, i),
                out_shape=jax.ShapeDtypeStruct((lines, 2 * bins, offsets), BF16),
                in_specs=[smem] + [any_space] * 3 + [vmem] * 2,
                out_specs=vmem,
                scratch_shapes=[
                    pltpu.VMEM((lines, offsets, depth), BF16),
                    pltpu.VMEM((lines, offsets, depth), BF16),
                    pltpu.VMEM((lines, offsets, depth), F32),
                    pltpu.VMEM((2, lines, offsets, depth), F32),
                    pltpu.VMEM((6, ROWS, depth), F32),
                    pltpu.VMEM((lines, offsets, depth), F32),
                    pltpu.SemaphoreType.DMA((3,)),
                ],
                cost_estimate=pl.CostEstimate(flops=3_000_000_000, bytes_accessed=0, transcendentals=0),
                compiler_params=pltpu.CompilerParams(vmem_limit_bytes=16 << 20),
            )(time_steps, halos[i], gathers, first if i < share else other, split, jnp.asarray(table))
        )
    rows = -(-inlines * lines // 16) * 16
    return pl.pallas_call(
        functools.partial(radon_kernel, near, apart),
        out_shape=jax.ShapeDtypeStruct((inlines, lines, offsets, depth), BF16),
        in_specs=[vmem] * (len(spectra) + 5),
        out_specs=vmem,
        scratch_shapes=[
            pltpu.VMEM((rows * 2 * bins, offsets), F32),
            pltpu.VMEM((rows * 2 * bins, offsets), F32),
        ],
        cost_estimate=pl.CostEstimate(flops=int(4e-6 * 1.0e15), bytes_accessed=0, transcendentals=0),
        compiler_params=pltpu.CompilerParams(vmem_limit_bytes=16 << 20),
        name="radon",
    )(*spectra, mine, theirs, mine_mate, theirs_mate, jnp.asarray(inverse_table(depth, bins)))


def solution(mesh):
    return jax.shard_map(
        swapped,
        mesh=mesh,
        in_specs=(P("parts", "xline", None, None), P(), P("xline", None, None, None)),
        out_specs=P("parts", "xline", None, None),
        check_vma=False,
    )
```

```python
import functools
import math

import jax
import jax.numpy as jnp
import numpy as np
from jax import lax
from jax.experimental import pallas as pl
from jax.experimental.pallas import tpu as pltpu
from jax.sharding import PartitionSpec as P

F32 = jnp.float32
BF16 = jnp.bfloat16
ROWS = 32


def forward_table(depth, bins):
    phase = (np.arange(depth)[:, None] * np.arange(bins)[None, :] % depth).astype(np.float32)
    phase = phase * np.float32(2.0 * math.pi / depth)
    return np.concatenate([np.cos(phase), -np.sin(phase)], axis=1).astype(BF16)


def inverse_table(depth, bins):
    phase = (np.arange(bins)[:, None] * np.arange(depth)[None, :] % depth).astype(np.float32)
    phase = phase * np.float32(2.0 * math.pi / depth)
    weight = np.where(np.arange(bins)[:, None] == 0, 1.0, 2.0).astype(np.float32) / np.float32(depth)
    return np.concatenate([weight * np.cos(phase), -weight * np.sin(phase)], axis=0).astype(BF16)


def split_matrix(depth):
    half = depth // 2
    source = np.concatenate([2 * np.arange(half), 2 * np.arange(half) + 1])
    return (np.arange(depth)[:, None] == source[None, :]).astype(BF16)


def shifts(half):
    lane = lax.broadcasted_iota(jnp.int32, (ROWS, half), 1)
    first, last = lane == 0, lane == half - 1
    zero = jnp.zeros((ROWS, half), BF16)

    def before(odd):
        return jnp.where(first, zero, pltpu.roll(odd, 1, 1))

    def after(even):
        return jnp.where(last, zero, pltpu.roll(even, half - 1, 1))

    return before, after


def step_lines(load, store, low, high, quarter, gate, before, after):
    narrow = {}

    def line(u):
        if u not in narrow:
            narrow[u] = tuple(part.astype(BF16) for part in load(u))
        return narrow[u]

    grads, prods, fluxes, slopes = {}, {}, {}, {}
    for u in range(low - 2, high + 2):
        (ae, ao), (be, bo), (ce, co) = line(u - 1), line(u), line(u + 1)
        gxe, gxo = ce - ae, co - ao
        if u == -1 and gate is not None:
            gxe, gxo = gxe * gate.astype(BF16), gxo * gate.astype(BF16)
        gze, gzo = bo - before(bo), after(be) - be
        grads[u] = gxe, gxo, gze, gzo
        prods[u] = (gxe * gxe, gxo * gxo, gxe * gze, gxo * gzo, gze * gze, gzo * gzo)
        v = u - 1
        if v - 1 in prods:
            sums = [a + b + c for a, b, c in zip(prods[v - 1], prods[v], prods[v + 1])]
            boxes = []
            for even, odd in zip(sums[0::2], sums[1::2]):
                both = even + odd
                boxes.append((both + before(odd), both + after(even)))
            gxe, gxo, gze, gzo = grads[v]
            flux = []
            for part, (gx, gz) in enumerate(((gxe, gze), (gxo, gzo))):
                sxx, sxz, szz = (box[part] for box in boxes)
                inverse = (1.0 / ((sxx + szz).astype(F32) + 36.0)).astype(BF16)
                flux.append((gx - (sxx * gx + sxz * gz) * inverse, gz - (sxz * gx + szz * gz) * inverse))
            (fxe, fze), (fxo, fzo) = flux
            fluxes[v] = fxe.astype(F32), fxo.astype(F32)
            slopes[v] = fzo.astype(F32) - before(fzo).astype(F32), after(fze).astype(F32) - fze.astype(F32)
        w = v - 1
        if low <= w < high:
            (fe, fo), (le, lo), (re, ro), (se, so) = load(w), fluxes[w - 1], fluxes[w + 1], slopes[w]
            fe = fe + quarter * ((re - le) + se)
            fo = fo + quarter * ((ro - lo) + so)
            if w == -1 and gate is not None:
                fe, fo = fe * gate, fo * gate
            store(w, fe, fo)


def place_of(flip, lines):
    def place(u):
        if u < 0:
            return 0, jnp.where(flip, -1 - u, lines + u)
        if u < lines:
            return 1, jnp.where(flip, lines - 1 - u, u)
        return 2, jnp.where(flip, 2 * lines - 1 - u, u - lines)

    return place


def strips(offsets, body):
    def run(s, carry):
        body(pl.ds(pl.multiple_of(s * ROWS, ROWS), ROWS))
        return carry

    lax.fori_loop(0, offsets // ROWS, run, 0)


def split_block(block, split):
    lines, offsets, depth = block.shape
    plain = jnp.dot(block.reshape(lines * offsets, depth), split, preferred_element_type=F32)
    return plain.reshape(lines, offsets, depth)


def inline_at(parity, turn, share):
    return jnp.where(parity == 1, (share + turn) % (2 * share), turn)


def early_kernel(tau_ref, own_ref, mate_ref, split_ref, out_ref, field_ref):
    _, lines, offsets, depth = own_ref.shape
    share = out_ref.shape[0]
    half = depth // 2
    parity = lax.axis_index("xline") % 2
    place = place_of(parity == 1, lines)
    places = {u: place(u) for u in range(2 * lines)}
    for i in range(share):
        at = parity * share + i
        field_ref[0] = split_block(own_ref[at], split_ref[...])
        field_ref[1] = split_block(mate_ref[at], split_ref[...])

        def strip(rows, i=i):
            before, after = shifts(half)

            def load(u):
                b, spot = places[u]
                return field_ref[b - 1, spot, rows, :half], field_ref[b - 1, spot, rows, half:]

            def store(u, even, odd):
                out_ref[i, u - 3, rows, :half] = even
                out_ref[i, u - 3, rows, half:] = odd

            step_lines(load, store, 3, lines + 3, tau_ref[0] * 0.25, None, before, after)

        strips(offsets, strip)


def late_kernel(turn, tau_ref, halo_ref, own_ref, first_ref, split_ref, table_ref, out_ref, field_ref, mid_ref, smooth_ref):
    lines, offsets, depth = own_ref.shape[1:]
    half = depth // 2
    share = first_ref.shape[0]
    me = lax.axis_index("xline")
    last = lax.axis_size("xline") - 1
    parity = me % 2
    gate = jnp.where((me == 0) | (me == last), 0.0, 1.0)
    mine = turn < share
    place = place_of(parity == 1, lines)
    places = {u: place(u) for u in range(-lines, lines)}
    field_ref[0] = split_block(halo_ref[0], split_ref[...])
    field_ref[1] = split_block(own_ref[inline_at(parity, turn, share)], split_ref[...])

    def strip(rows):
        before, after = shifts(half)

        def load(u):
            b, spot = places[u]
            return field_ref[b, spot, rows, :half], field_ref[b, spot, rows, half:]

        def keep(u, even, odd):
            mid_ref[u + 3, :, :half] = even
            mid_ref[u + 3, :, half:] = odd

        def fetch(u):
            if u < 3:
                return mid_ref[u + 3, :, :half], mid_ref[u + 3, :, half:]
            spot = u - 3 if mine else lines + 2 - u
            return first_ref[turn % share, spot, rows, :half], first_ref[turn % share, spot, rows, half:]

        def store(u, even, odd):
            spot = places[u][1]
            smooth_ref[spot, rows, :half] = even
            smooth_ref[spot, rows, half:] = odd

        step_lines(load, keep, -3, 3, tau_ref[0] * 0.25, gate, before, after)
        step_lines(fetch, store, 0, lines, tau_ref[1] * 0.25, gate, before, after)

    strips(offsets, strip)
    for x in range(lines):
        smooth = smooth_ref[x].astype(BF16)
        spectrum = lax.dot_general(table_ref[...], smooth, (((1,), (1,)), ((), ())), preferred_element_type=F32)
        out_ref[x] = spectrum.astype(BF16)


def stage_bins(spec_refs, bins_ref):
    lines, twice = spec_refs[0].shape[:2]
    for i, spec_ref in enumerate(spec_refs):
        for x in range(lines):
            at = (i * lines + x) * twice
            bins_ref[at : at + twice, :] = spec_ref[x].astype(F32)


def bins_of(near, apart, planes, extras, held):
    me = lax.axis_index("xline") ^ (apart * (lax.axis_index("parts") % planes))
    return [
        (n, j, b, (me ^ (offset ^ extra)) * held + b)
        for n, extra in enumerate(extras)
        for j, offset in enumerate(near)
        for b in range(held)
    ]


def filter_bin(bins_ref, twice, k, by_real_ref, by_imag_ref):
    rows = bins_ref.shape[0] // twice
    real = bins_ref[pl.ds(k, rows, stride=twice), :]
    imag = bins_ref[pl.ds(twice // 2 + k, rows, stride=twice), :]
    both = jnp.concatenate([real, imag], axis=0).astype(BF16)
    by_real = lax.dot_general(both, by_real_ref[...], (((1,), (1,)), ((), ())), preferred_element_type=F32)
    by_imag = lax.dot_general(both, by_imag_ref[...], (((1,), (1,)), ((), ())), preferred_element_type=F32)
    return by_real[:rows] - by_imag[rows:], by_imag[:rows] + by_real[rows:]


def some_bins_kernel(near, apart, planes, extras, *refs):
    *spec_refs, out_ref, bins_ref = refs
    spec_refs, set_refs = spec_refs[: -len(extras)], spec_refs[-len(extras) :]
    twice = spec_refs[0].shape[1]
    stage_bins(spec_refs, bins_ref)
    for at, (n, j, b, k) in enumerate(bins_of(near, apart, planes, extras, set_refs[0].shape[1])):
        ref = set_refs[n]
        out_ref[at, 0], out_ref[at, 1] = filter_bin(bins_ref, twice, k, ref.at[j, b, 0], ref.at[j, b, 1])


def radon_kernel(near, apart, planes, extras, last_extra, *refs):
    *spec_refs, some_ref, last_ref, inverse_ref, out_hbm, bins_ref, done_ref, out_ref, sems = refs
    lines, twice = spec_refs[0].shape[:2]
    bins = twice // 2
    rows = bins_ref.shape[0] // twice
    held = last_ref.shape[1]
    parity = lax.axis_index("xline") % 2
    for at, (_, _, _, k) in enumerate(bins_of(near, apart, planes, extras, held)):
        done_ref[pl.ds(k, rows, stride=twice), :] = some_ref[at, 0]
        done_ref[pl.ds(bins + k, rows, stride=twice), :] = some_ref[at, 1]
    stage_bins(spec_refs, bins_ref)
    for _, j, b, k in bins_of(near, apart, planes, (last_extra,), held):
        real, imag = filter_bin(bins_ref, twice, k, last_ref.at[j, b, 0], last_ref.at[j, b, 1])
        done_ref[pl.ds(k, rows, stride=twice), :] = real
        done_ref[pl.ds(bins + k, rows, stride=twice), :] = imag
    copies = []
    for i in range(len(spec_refs)):
        inline = inline_at(parity, i, len(spec_refs) // 2)
        for x in range(lines):
            at = (i * lines + x) * twice
            filtered = done_ref[at : at + twice, :].astype(BF16)
            result = lax.dot_general(filtered, inverse_ref[...], (((0,), (0,)), ((), ())), preferred_element_type=F32)
            out_ref[i, x] = result.astype(BF16)
            copy = pltpu.make_async_copy(out_ref.at[i, x], out_hbm.at[inline, x], sems.at[i, x])
            copy.start()
            copies.append(copy)
    for copy in copies:
        copy.wait()


def swapped(gathers, time_steps, radon_op):
    inlines, lines, offsets, depth = gathers.shape
    devices = lax.axis_size("xline")
    held = radon_op.shape[0]
    bins = held * devices
    planes = 1
    apart = 4
    near = tuple(o for o in range(0, devices, 2) if not o & apart)

    def swap(value, mask):
        return lax.ppermute(value, "xline", [(i, i ^ mask) for i in range(devices)])

    cross = [(i, i + 1) for i in range(1, devices - 1, 2)] + [(i + 1, i) for i in range(1, devices - 1, 2)]
    pieces = [radon_op]
    for o in reversed(near[1:]):
        pieces.append(swap(radon_op, o))
    pieces = [pieces[0]] + pieces[:0:-1]
    mate = swap(gathers, 1)
    halos = []
    for i in range(inlines):
        at = inline_at(1 - lax.axis_index("xline") % 2, i, inlines // 2)
        sent = lax.dynamic_slice_in_dim(gathers, at, 1, axis=0)
        halos.append(lax.ppermute(sent, "xline", cross))
    mine = jnp.stack(pieces)
    theirs = swap(mine, apart)
    mine_mate = swap(mine, 1)
    theirs_mate = swap(theirs, 1)

    vmem = pl.BlockSpec(memory_space=pltpu.VMEM)
    smem = pl.BlockSpec(memory_space=pltpu.SMEM)
    table = forward_table(depth, bins)
    table = np.concatenate([table[0::2], table[1::2]], axis=0).T
    split = jnp.asarray(split_matrix(depth))
    any_space = pl.BlockSpec(memory_space=pltpu.HBM)
    share = inlines // 2
    first = pl.pallas_call(
        early_kernel,
        out_shape=jax.ShapeDtypeStruct((share, lines, offsets, depth), F32),
        in_specs=[smem] + [vmem] * 3,
        out_specs=vmem,
        scratch_shapes=[pltpu.VMEM((2, lines, offsets, depth), F32)],
        cost_estimate=pl.CostEstimate(flops=3_000_000_000, bytes_accessed=0, transcendentals=0),
        compiler_params=pltpu.CompilerParams(vmem_limit_bytes=16 << 20),
        name="early",
    )(time_steps, gathers, mate, split)
    other = swap(first, 1)
    spectra = []
    for i in range(inlines):
        spectra.append(
            pl.pallas_call(
                functools.partial(late_kernel, i),
                out_shape=jax.ShapeDtypeStruct((lines, 2 * bins, offsets), BF16),
                in_specs=[smem] + [vmem] * 5,
                out_specs=vmem,
                scratch_shapes=[
                    pltpu.VMEM((2, lines, offsets, depth), F32),
                    pltpu.VMEM((6, ROWS, depth), F32),
                    pltpu.VMEM((lines, offsets, depth), F32),
                ],
                cost_estimate=pl.CostEstimate(flops=3_000_000_000, bytes_accessed=0, transcendentals=0),
                compiler_params=pltpu.CompilerParams(vmem_limit_bytes=16 << 20),
            )(time_steps, halos[i], gathers, first if i < share else other, split, jnp.asarray(table))
        )
    rows = -(-inlines * lines // 16) * 16
    extras = (0, 1, apart)
    some = pl.pallas_call(
        functools.partial(some_bins_kernel, near, apart, planes, extras),
        out_shape=jax.ShapeDtypeStruct((len(extras) * len(near) * held, 2, rows, offsets), F32),
        in_specs=[vmem] * (len(spectra) + len(extras)),
        out_specs=vmem,
        scratch_shapes=[pltpu.VMEM((rows * 2 * bins, offsets), F32)],
        cost_estimate=pl.CostEstimate(flops=1_000_000_000, bytes_accessed=0, transcendentals=0),
        compiler_params=pltpu.CompilerParams(vmem_limit_bytes=16 << 20),
        name="some",
    )(*spectra, mine, mine_mate, theirs)
    return pl.pallas_call(
        functools.partial(radon_kernel, near, apart, planes, extras, 1 ^ apart),
        out_shape=jax.ShapeDtypeStruct((inlines, lines, offsets, depth), BF16),
        in_specs=[vmem] * (len(spectra) + 3),
        out_specs=any_space,
        scratch_shapes=[
            pltpu.VMEM((rows * 2 * bins, offsets), F32),
            pltpu.VMEM((rows * 2 * bins, offsets), F32),
            pltpu.VMEM((inlines, lines, offsets, depth), BF16),
            pltpu.SemaphoreType.DMA((inlines, lines)),
        ],
        cost_estimate=pl.CostEstimate(flops=2_000_000_000, bytes_accessed=0, transcendentals=0),
        compiler_params=pltpu.CompilerParams(vmem_limit_bytes=16 << 20),
        name="radon",
    )(*spectra, some, theirs_mate, jnp.asarray(inverse_table(depth, bins)))


def solution(mesh):
    return jax.shard_map(
        swapped,
        mesh=mesh,
        in_specs=(P("parts", "xline", None, None), P(), P("xline", None, None, None)),
        out_specs=P("parts", "xline", None, None),
        check_vma=False,
    )
```

```python
import functools
import math

import jax
import jax.numpy as jnp
import numpy as np
from jax import lax
from jax.experimental import pallas as pl
from jax.experimental.pallas import tpu as pltpu
from jax.sharding import PartitionSpec as P

F32 = jnp.float32
BF16 = jnp.bfloat16
ROWS = 32


def forward_table(depth, bins):
    phase = (np.arange(depth)[:, None] * np.arange(bins)[None, :] % depth).astype(np.float32)
    phase = phase * np.float32(2.0 * math.pi / depth)
    return np.concatenate([np.cos(phase), -np.sin(phase)], axis=1).astype(BF16)


def inverse_table(depth, bins):
    phase = (np.arange(bins)[:, None] * np.arange(depth)[None, :] % depth).astype(np.float32)
    phase = phase * np.float32(2.0 * math.pi / depth)
    weight = np.where(np.arange(bins)[:, None] == 0, 1.0, 2.0).astype(np.float32) / np.float32(depth)
    return np.concatenate([weight * np.cos(phase), -weight * np.sin(phase)], axis=0).astype(BF16)


def split_matrix(depth):
    half = depth // 2
    source = np.concatenate([2 * np.arange(half), 2 * np.arange(half) + 1])
    return (np.arange(depth)[:, None] == source[None, :]).astype(BF16)


def shifts(half):
    lane = lax.broadcasted_iota(jnp.int32, (ROWS, half), 1)
    first, last = lane == 0, lane == half - 1
    zero = jnp.zeros((ROWS, half), BF16)

    def before(odd):
        return jnp.where(first, zero, pltpu.roll(odd, 1, 1))

    def after(even):
        return jnp.where(last, zero, pltpu.roll(even, half - 1, 1))

    return before, after


def step_lines(load, store, low, high, quarter, gate, before, after):
    narrow = {}

    def line(u):
        if u not in narrow:
            narrow[u] = tuple(part.astype(BF16) for part in load(u))
        return narrow[u]

    grads, prods, fluxes, slopes = {}, {}, {}, {}
    for u in range(low - 2, high + 2):
        (ae, ao), (be, bo), (ce, co) = line(u - 1), line(u), line(u + 1)
        gxe, gxo = ce - ae, co - ao
        if u == -1 and gate is not None:
            gxe, gxo = gxe * gate.astype(BF16), gxo * gate.astype(BF16)
        gze, gzo = bo - before(bo), after(be) - be
        grads[u] = gxe, gxo, gze, gzo
        prods[u] = (gxe * gxe, gxo * gxo, gxe * gze, gxo * gzo, gze * gze, gzo * gzo)
        v = u - 1
        if v - 1 in prods:
            sums = [a + b + c for a, b, c in zip(prods[v - 1], prods[v], prods[v + 1])]
            boxes = []
            for even, odd in zip(sums[0::2], sums[1::2]):
                both = even + odd
                boxes.append((both + before(odd), both + after(even)))
            gxe, gxo, gze, gzo = grads[v]
            flux = []
            for part, (gx, gz) in enumerate(((gxe, gze), (gxo, gzo))):
                sxx, sxz, szz = (box[part] for box in boxes)
                inverse = (1.0 / ((sxx + szz).astype(F32) + 36.0)).astype(BF16)
                flux.append((gx - (sxx * gx + sxz * gz) * inverse, gz - (sxz * gx + szz * gz) * inverse))
            (fxe, fze), (fxo, fzo) = flux
            fluxes[v] = fxe.astype(F32), fxo.astype(F32)
            slopes[v] = fzo.astype(F32) - before(fzo).astype(F32), after(fze).astype(F32) - fze.astype(F32)
        w = v - 1
        if low <= w < high:
            (fe, fo), (le, lo), (re, ro), (se, so) = load(w), fluxes[w - 1], fluxes[w + 1], slopes[w]
            fe = fe + quarter * ((re - le) + se)
            fo = fo + quarter * ((ro - lo) + so)
            if w == -1 and gate is not None:
                fe, fo = fe * gate, fo * gate
            store(w, fe, fo)


def place_of(flip, lines):
    def place(u):
        if u < 0:
            return 0, jnp.where(flip, -1 - u, lines + u)
        if u < lines:
            return 1, jnp.where(flip, lines - 1 - u, u)
        return 2, jnp.where(flip, 2 * lines - 1 - u, u - lines)

    return place


def strips(offsets, body):
    def run(s, carry):
        body(pl.ds(pl.multiple_of(s * ROWS, ROWS), ROWS))
        return carry

    lax.fori_loop(0, offsets // ROWS, run, 0)


def split_block(block, split):
    lines, offsets, depth = block.shape
    plain = jnp.dot(block.reshape(lines * offsets, depth), split, preferred_element_type=F32)
    return plain.reshape(lines, offsets, depth)


def inline_at(parity, turn, share):
    return jnp.where(parity == 1, (share + turn) % (2 * share), turn)


def early_kernel(tau_ref, own_ref, mate_ref, split_ref, out_ref, field_ref):
    _, lines, offsets, depth = own_ref.shape
    share = out_ref.shape[0]
    half = depth // 2
    parity = lax.axis_index("xline") % 2
    place = place_of(parity == 1, lines)
    places = {u: place(u) for u in range(2 * lines)}
    for i in range(share):
        at = parity * share + i
        field_ref[0] = split_block(own_ref[at], split_ref[...])
        field_ref[1] = split_block(mate_ref[at], split_ref[...])

        def strip(rows, i=i):
            before, after = shifts(half)

            def load(u):
                b, spot = places[u]
                return field_ref[b - 1, spot, rows, :half], field_ref[b - 1, spot, rows, half:]

            def store(u, even, odd):
                out_ref[i, u - 3, rows, :half] = even
                out_ref[i, u - 3, rows, half:] = odd

            step_lines(load, store, 3, lines + 3, tau_ref[0] * 0.25, None, before, after)

        strips(offsets, strip)


def late_kernel(turn, tau_ref, halo_ref, own_ref, first_ref, split_ref, table_ref, out_ref, field_ref, mid_ref, smooth_ref):
    lines, offsets, depth = own_ref.shape[1:]
    half = depth // 2
    share = first_ref.shape[0]
    me = lax.axis_index("xline")
    last = lax.axis_size("xline") - 1
    parity = me % 2
    gate = jnp.where((me == 0) | (me == last), 0.0, 1.0)
    mine = turn < share
    place = place_of(parity == 1, lines)
    places = {u: place(u) for u in range(-lines, lines)}
    field_ref[0] = split_block(halo_ref[0], split_ref[...])
    field_ref[1] = split_block(own_ref[inline_at(parity, turn, share)], split_ref[...])

    def strip(rows):
        before, after = shifts(half)

        def load(u):
            b, spot = places[u]
            return field_ref[b, spot, rows, :half], field_ref[b, spot, rows, half:]

        def keep(u, even, odd):
            mid_ref[u + 3, :, :half] = even
            mid_ref[u + 3, :, half:] = odd

        def fetch(u):
            if u < 3:
                return mid_ref[u + 3, :, :half], mid_ref[u + 3, :, half:]
            spot = u - 3 if mine else lines + 2 - u
            return first_ref[turn % share, spot, rows, :half], first_ref[turn % share, spot, rows, half:]

        def store(u, even, odd):
            spot = places[u][1]
            smooth_ref[spot, rows, :half] = even
            smooth_ref[spot, rows, half:] = odd

        step_lines(load, keep, -3, 3, tau_ref[0] * 0.25, gate, before, after)
        step_lines(fetch, store, 0, lines, tau_ref[1] * 0.25, gate, before, after)

    strips(offsets, strip)
    for x in range(lines):
        smooth = smooth_ref[x].astype(BF16)
        spectrum = lax.dot_general(table_ref[...], smooth, (((1,), (1,)), ((), ())), preferred_element_type=F32)
        out_ref[x] = spectrum.astype(BF16)


def radon_kernel(near, apart, planes, *refs):
    *spec_refs, mine_ref, theirs_ref, mine_mate_ref, theirs_mate_ref, inverse_ref, out_hbm, bins_ref, done_ref, out_ref, sems = refs
    lines, twice, _ = spec_refs[0].shape
    bins = twice // 2
    rows = bins_ref.shape[0] // twice
    me = lax.axis_index("xline")
    parity = me % 2
    for i, spec_ref in enumerate(spec_refs):
        for x in range(lines):
            at = (i * lines + x) * twice
            bins_ref[at : at + twice, :] = spec_ref[x].astype(F32)
    held = mine_ref.shape[1]
    me = me ^ (apart * (lax.axis_index("parts") % planes))
    for ref, extra in ((mine_ref, 0), (mine_mate_ref, 1), (theirs_ref, apart), (theirs_mate_ref, 1 ^ apart)):
        for j, offset in enumerate(near):
            owner = me ^ (offset ^ extra)
            for b in range(held):
                k = owner * held + b
                real = bins_ref[pl.ds(k, rows, stride=twice), :]
                imag = bins_ref[pl.ds(bins + k, rows, stride=twice), :]
                both = jnp.concatenate([real, imag], axis=0).astype(BF16)
                by_real = lax.dot_general(both, ref[j, b, 0], (((1,), (1,)), ((), ())), preferred_element_type=F32)
                by_imag = lax.dot_general(both, ref[j, b, 1], (((1,), (1,)), ((), ())), preferred_element_type=F32)
                done_ref[pl.ds(k, rows, stride=twice), :] = by_real[:rows] - by_imag[rows:]
                done_ref[pl.ds(bins + k, rows, stride=twice), :] = by_imag[:rows] + by_real[rows:]
    copies = []
    for i in range(len(spec_refs)):
        inline = inline_at(parity, i, len(spec_refs) // 2)
        for x in range(lines):
            at = (i * lines + x) * twice
            filtered = done_ref[at : at + twice, :].astype(BF16)
            result = lax.dot_general(filtered, inverse_ref[...], (((0,), (0,)), ((), ())), preferred_element_type=F32)
            out_ref[i, x] = result.astype(BF16)
            copy = pltpu.make_async_copy(out_ref.at[i, x], out_hbm.at[inline, x], sems.at[i, x])
            copy.start()
            copies.append(copy)
    for copy in copies:
        copy.wait()


def swapped(gathers, time_steps, radon_op):
    inlines, lines, offsets, depth = gathers.shape
    devices = lax.axis_size("xline")
    held = radon_op.shape[0]
    bins = held * devices
    parts = lax.axis_size("parts")
    planes = 2 if parts % 2 == 0 else 1
    apart = 4
    near = tuple(o for o in range(0, devices, 2) if not o & apart)

    def swap(value, mask):
        return lax.ppermute(value, "xline", [(i, i ^ mask) for i in range(devices)])

    cross = [(i, i + 1) for i in range(1, devices - 1, 2)] + [(i + 1, i) for i in range(1, devices - 1, 2)]
    plane = lax.axis_index("parts") % planes
    pieces = []
    for o in reversed(near):
        pairs = [
            (q * devices + i, q * devices + (i ^ o ^ (apart * (q % planes)) if o else i ^ apart))
            for q in range(parts)
            for i in range(devices)
        ]
        pieces.append(lax.ppermute(radon_op, ("parts", "xline"), pairs))
    pieces = pieces[::-1]
    pieces[0] = jnp.where(plane == 0, radon_op, pieces[0])
    mate = swap(gathers, 1)
    halos = []
    for i in range(inlines):
        at = inline_at(1 - lax.axis_index("xline") % 2, i, inlines // 2)
        sent = lax.dynamic_slice_in_dim(gathers, at, 1, axis=0)
        halos.append(lax.ppermute(sent, "xline", cross))
    mine = jnp.stack(pieces)
    if planes == 2:
        pairs = [(q * devices + i, (q ^ 1) * devices + i) for q in range(parts) for i in range(devices)]
        theirs = lax.ppermute(mine, ("parts", "xline"), pairs)
    else:
        theirs = swap(mine, apart)
    mine_mate = swap(mine, 1)
    theirs_mate = swap(theirs, 1)

    vmem = pl.BlockSpec(memory_space=pltpu.VMEM)
    smem = pl.BlockSpec(memory_space=pltpu.SMEM)
    table = forward_table(depth, bins)
    table = np.concatenate([table[0::2], table[1::2]], axis=0).T
    split = jnp.asarray(split_matrix(depth))
    any_space = pl.BlockSpec(memory_space=pltpu.HBM)
    share = inlines // 2
    first = pl.pallas_call(
        early_kernel,
        out_shape=jax.ShapeDtypeStruct((share, lines, offsets, depth), F32),
        in_specs=[smem] + [vmem] * 3,
        out_specs=vmem,
        scratch_shapes=[pltpu.VMEM((2, lines, offsets, depth), F32)],
        cost_estimate=pl.CostEstimate(flops=3_000_000_000, bytes_accessed=0, transcendentals=0),
        compiler_params=pltpu.CompilerParams(vmem_limit_bytes=16 << 20),
        name="early",
    )(time_steps, gathers, mate, split)
    other = swap(first, 1)
    spectra = []
    for i in range(inlines):
        spectra.append(
            pl.pallas_call(
                functools.partial(late_kernel, i),
                out_shape=jax.ShapeDtypeStruct((lines, 2 * bins, offsets), BF16),
                in_specs=[smem] + [vmem] * 5,
                out_specs=vmem,
                scratch_shapes=[
                    pltpu.VMEM((2, lines, offsets, depth), F32),
                    pltpu.VMEM((6, ROWS, depth), F32),
                    pltpu.VMEM((lines, offsets, depth), F32),
                ],
                cost_estimate=pl.CostEstimate(flops=3_000_000_000, bytes_accessed=0, transcendentals=0),
                compiler_params=pltpu.CompilerParams(vmem_limit_bytes=16 << 20),
            )(time_steps, halos[i], gathers, first if i < share else other, split, jnp.asarray(table))
        )
    rows = -(-inlines * lines // 16) * 16
    return pl.pallas_call(
        functools.partial(radon_kernel, near, apart, planes),
        out_shape=jax.ShapeDtypeStruct((inlines, lines, offsets, depth), BF16),
        in_specs=[vmem] * (len(spectra) + 5),
        out_specs=any_space,
        scratch_shapes=[
            pltpu.VMEM((rows * 2 * bins, offsets), F32),
            pltpu.VMEM((rows * 2 * bins, offsets), F32),
            pltpu.VMEM((inlines, lines, offsets, depth), BF16),
            pltpu.SemaphoreType.DMA((inlines, lines)),
        ],
        cost_estimate=pl.CostEstimate(flops=int(4e-6 * 1.0e15), bytes_accessed=0, transcendentals=0),
        compiler_params=pltpu.CompilerParams(vmem_limit_bytes=16 << 20),
        name="radon",
    )(*spectra, mine, theirs, mine_mate, theirs_mate, jnp.asarray(inverse_table(depth, bins)))


def solution(mesh):
    return jax.shard_map(
        swapped,
        mesh=mesh,
        in_specs=(P("parts", "xline", None, None), P(), P("xline", None, None, None)),
        out_specs=P("parts", "xline", None, None),
        check_vma=False,
    )
```

```python
import functools
import math

import jax
import jax.numpy as jnp
import numpy as np
from jax import lax
from jax.experimental import pallas as pl
from jax.experimental.pallas import tpu as pltpu
from jax.sharding import PartitionSpec as P

F32 = jnp.float32
BF16 = jnp.bfloat16
ROWS = 32


def forward_table(depth, bins):
    phase = (np.arange(depth)[:, None] * np.arange(bins)[None, :] % depth).astype(np.float32)
    phase = phase * np.float32(2.0 * math.pi / depth)
    return np.concatenate([np.cos(phase), -np.sin(phase)], axis=1).astype(BF16)


def inverse_table(depth, bins):
    phase = (np.arange(bins)[:, None] * np.arange(depth)[None, :] % depth).astype(np.float32)
    phase = phase * np.float32(2.0 * math.pi / depth)
    weight = np.where(np.arange(bins)[:, None] == 0, 1.0, 2.0).astype(np.float32) / np.float32(depth)
    return np.concatenate([weight * np.cos(phase), -weight * np.sin(phase)], axis=0).astype(BF16)


def split_matrix(depth):
    half = depth // 2
    source = np.concatenate([2 * np.arange(half), 2 * np.arange(half) + 1])
    return (np.arange(depth)[:, None] == source[None, :]).astype(BF16)


def shifts(half):
    lane = lax.broadcasted_iota(jnp.int32, (ROWS, half), 1)
    first, last = lane == 0, lane == half - 1
    zero = jnp.zeros((ROWS, half), BF16)

    def before(odd):
        return jnp.where(first, zero, pltpu.roll(odd, 1, 1))

    def after(even):
        return jnp.where(last, zero, pltpu.roll(even, half - 1, 1))

    return before, after


def step_lines(load, store, low, high, quarter, gate, before, after):
    narrow = {}

    def line(u):
        if u not in narrow:
            narrow[u] = tuple(part.astype(BF16) for part in load(u))
        return narrow[u]

    grads, prods, pairs, fluxes, slopes = {}, {}, {}, {}, {}
    for u in range(low - 2, high + 2):
        (ae, ao), (be, bo), (ce, co) = line(u - 1), line(u), line(u + 1)
        gxe, gxo = ce - ae, co - ao
        if u == -1 and gate is not None:
            gxe, gxo = gxe * gate.astype(BF16), gxo * gate.astype(BF16)
        gze, gzo = bo - before(bo), after(be) - be
        grads[u] = gxe, gxo, gze, gzo
        prods[u] = (gxe * gxe, gxo * gxo, gxe * gze, gxo * gzo, gze * gze, gzo * gzo)
        v = u - 1
        if v - 1 in prods:
            first = v - v % 2
            if first not in pairs:
                pairs[first] = [a + b for a, b in zip(prods[first], prods[first + 1])]
            sums = [a + b for a, b in zip(pairs[first], prods[v - 1 if v == first else v + 1])]
            boxes = []
            for even, odd in zip(sums[0::2], sums[1::2]):
                both = even + odd
                boxes.append((both + before(odd), both + after(even)))
            gxe, gxo, gze, gzo = grads[v]
            flux = []
            for part, (gx, gz) in enumerate(((gxe, gze), (gxo, gzo))):
                sxx, sxz, szz = (box[part] for box in boxes)
                inverse = (1.0 / ((sxx + szz).astype(F32) + 36.0)).astype(BF16)
                flux.append((gx - (sxx * gx + sxz * gz) * inverse, gz - (sxz * gx + szz * gz) * inverse))
            (fxe, fze), (fxo, fzo) = flux
            fluxes[v] = fxe.astype(F32), fxo.astype(F32)
            slopes[v] = fzo.astype(F32) - before(fzo).astype(F32), after(fze).astype(F32) - fze.astype(F32)
        w = v - 1
        if low <= w < high:
            (fe, fo), (le, lo), (re, ro), (se, so) = load(w), fluxes[w - 1], fluxes[w + 1], slopes[w]
            fe = fe + quarter * ((re - le) + se)
            fo = fo + quarter * ((ro - lo) + so)
            if w == -1 and gate is not None:
                fe, fo = fe * gate, fo * gate
            store(w, fe, fo)


def place_of(flip, lines):
    def place(u):
        if u < 0:
            return 0, jnp.where(flip, -1 - u, lines + u)
        if u < lines:
            return 1, jnp.where(flip, lines - 1 - u, u)
        return 2, jnp.where(flip, 2 * lines - 1 - u, u - lines)

    return place


def strips(offsets, body):
    def run(s, carry):
        body(pl.ds(pl.multiple_of(s * ROWS, ROWS), ROWS))
        return carry

    lax.fori_loop(0, offsets // ROWS, run, 0)


def split_block(block, split):
    lines, offsets, depth = block.shape
    plain = jnp.dot(block.reshape(lines * offsets, depth), split, preferred_element_type=F32)
    return plain.reshape(lines, offsets, depth)


def inline_at(parity, turn, share):
    return jnp.where(parity == 1, (share + turn) % (2 * share), turn)


def early_kernel(tau_ref, own_ref, mate_ref, split_ref, out_ref, field_ref):
    _, lines, offsets, depth = own_ref.shape
    share = out_ref.shape[0]
    half = depth // 2
    parity = lax.axis_index("xline") % 2
    place = place_of(parity == 1, lines)
    places = {u: place(u) for u in range(2 * lines)}
    for i in range(share):
        at = parity * share + i
        field_ref[0] = split_block(own_ref[at], split_ref[...])
        field_ref[1] = split_block(mate_ref[at], split_ref[...])

        def strip(rows, i=i):
            before, after = shifts(half)

            def load(u):
                b, spot = places[u]
                return field_ref[b - 1, spot, rows, :half], field_ref[b - 1, spot, rows, half:]

            def store(u, even, odd):
                out_ref[i, u - 3, rows, :half] = even
                out_ref[i, u - 3, rows, half:] = odd

            step_lines(load, store, 3, lines + 3, tau_ref[0] * 0.25, None, before, after)

        strips(offsets, strip)


def late_kernel(turn, tau_ref, halo_ref, own_ref, first_ref, split_ref, table_ref, out_ref, field_ref, mid_ref, smooth_ref):
    lines, offsets, depth = own_ref.shape[1:]
    half = depth // 2
    share = first_ref.shape[0]
    me = lax.axis_index("xline")
    last = lax.axis_size("xline") - 1
    parity = me % 2
    gate = jnp.where((me == 0) | (me == last), 0.0, 1.0)
    mine = turn < share
    place = place_of(parity == 1, lines)
    places = {u: place(u) for u in range(-lines, lines)}
    field_ref[0] = split_block(halo_ref[0], split_ref[...])
    field_ref[1] = split_block(own_ref[inline_at(parity, turn, share)], split_ref[...])

    def strip(rows):
        before, after = shifts(half)

        def load(u):
            b, spot = places[u]
            return field_ref[b, spot, rows, :half], field_ref[b, spot, rows, half:]

        def keep(u, even, odd):
            mid_ref[u + 3, :, :half] = even
            mid_ref[u + 3, :, half:] = odd

        def fetch(u):
            if u < 3:
                return mid_ref[u + 3, :, :half], mid_ref[u + 3, :, half:]
            spot = u - 3 if mine else lines + 2 - u
            return first_ref[turn % share, spot, rows, :half], first_ref[turn % share, spot, rows, half:]

        def store(u, even, odd):
            spot = places[u][1]
            smooth_ref[spot, rows, :half] = even
            smooth_ref[spot, rows, half:] = odd

        step_lines(load, keep, -3, 3, tau_ref[0] * 0.25, gate, before, after)
        step_lines(fetch, store, 0, lines, tau_ref[1] * 0.25, gate, before, after)

    strips(offsets, strip)
    for x in range(lines):
        smooth = smooth_ref[x].astype(BF16)
        spectrum = lax.dot_general(table_ref[...], smooth, (((1,), (1,)), ((), ())), preferred_element_type=F32)
        out_ref[x] = spectrum.astype(BF16)


def radon_kernel(near, apart, planes, *refs):
    *spec_refs, mine_ref, theirs_ref, mine_mate_ref, theirs_mate_ref, inverse_ref, out_hbm, bins_ref, done_ref, out_ref, sems = refs
    lines, twice, _ = spec_refs[0].shape
    bins = twice // 2
    rows = bins_ref.shape[0] // twice
    me = lax.axis_index("xline")
    parity = me % 2
    for i, spec_ref in enumerate(spec_refs):
        for x in range(lines):
            at = (i * lines + x) * twice
            bins_ref[at : at + twice, :] = spec_ref[x].astype(F32)
    held = mine_ref.shape[1]
    me = me ^ (apart * (lax.axis_index("parts") % planes))
    for ref, extra in ((mine_ref, 0), (mine_mate_ref, 1), (theirs_ref, apart), (theirs_mate_ref, 1 ^ apart)):
        for j, offset in enumerate(near):
            owner = me ^ (offset ^ extra)
            for b in range(held):
                k = owner * held + b
                real = bins_ref[pl.ds(k, rows, stride=twice), :]
                imag = bins_ref[pl.ds(bins + k, rows, stride=twice), :]
                both = jnp.concatenate([real, imag], axis=0).astype(BF16)
                by_real = lax.dot_general(both, ref[j, b, 0], (((1,), (1,)), ((), ())), preferred_element_type=F32)
                by_imag = lax.dot_general(both, ref[j, b, 1], (((1,), (1,)), ((), ())), preferred_element_type=F32)
                done_ref[pl.ds(k, rows, stride=twice), :] = by_real[:rows] - by_imag[rows:]
                done_ref[pl.ds(bins + k, rows, stride=twice), :] = by_imag[:rows] + by_real[rows:]
    copies = []
    for i in range(len(spec_refs)):
        inline = inline_at(parity, i, len(spec_refs) // 2)
        for x in range(lines):
            at = (i * lines + x) * twice
            filtered = done_ref[at : at + twice, :].astype(BF16)
            result = lax.dot_general(filtered, inverse_ref[...], (((0,), (0,)), ((), ())), preferred_element_type=F32)
            out_ref[i, x] = result.astype(BF16)
            copy = pltpu.make_async_copy(out_ref.at[i, x], out_hbm.at[inline, x], sems.at[i, x])
            copy.start()
            copies.append(copy)
    for copy in copies:
        copy.wait()


def swapped(gathers, time_steps, radon_op):
    inlines, lines, offsets, depth = gathers.shape
    devices = lax.axis_size("xline")
    held = radon_op.shape[0]
    bins = held * devices
    parts = lax.axis_size("parts")
    planes = 2 if parts % 2 == 0 else 1
    apart = 4
    near = tuple(o for o in range(0, devices, 2) if not o & apart)

    def swap(value, mask):
        return lax.ppermute(value, "xline", [(i, i ^ mask) for i in range(devices)])

    cross = [(i, i + 1) for i in range(1, devices - 1, 2)] + [(i + 1, i) for i in range(1, devices - 1, 2)]
    plane = lax.axis_index("parts") % planes
    pieces = []
    for o in reversed(near):
        pairs = [
            (q * devices + i, q * devices + (i ^ o ^ (apart * (q % planes)) if o else i ^ apart))
            for q in range(parts)
            for i in range(devices)
        ]
        pieces.append(lax.ppermute(radon_op, ("parts", "xline"), pairs))
    pieces = pieces[::-1]
    pieces[0] = jnp.where(plane == 0, radon_op, pieces[0])
    mate = swap(gathers, 1)
    halos = []
    for i in range(inlines):
        at = inline_at(1 - lax.axis_index("xline") % 2, i, inlines // 2)
        sent = lax.dynamic_slice_in_dim(gathers, at, 1, axis=0)
        halos.append(lax.ppermute(sent, "xline", cross))
    mine = jnp.stack(pieces)
    if planes == 2:
        pairs = [(q * devices + i, (q ^ 1) * devices + i) for q in range(parts) for i in range(devices)]
        theirs = lax.ppermute(mine, ("parts", "xline"), pairs)
    else:
        theirs = swap(mine, apart)
    mine_mate = swap(mine, 1)
    theirs_mate = swap(theirs, 1)

    vmem = pl.BlockSpec(memory_space=pltpu.VMEM)
    smem = pl.BlockSpec(memory_space=pltpu.SMEM)
    table = forward_table(depth, bins)
    table = np.concatenate([table[0::2], table[1::2]], axis=0).T
    split = jnp.asarray(split_matrix(depth))
    any_space = pl.BlockSpec(memory_space=pltpu.HBM)
    share = inlines // 2
    first = pl.pallas_call(
        early_kernel,
        out_shape=jax.ShapeDtypeStruct((share, lines, offsets, depth), F32),
        in_specs=[smem] + [vmem] * 3,
        out_specs=vmem,
        scratch_shapes=[pltpu.VMEM((2, lines, offsets, depth), F32)],
        cost_estimate=pl.CostEstimate(flops=3_000_000_000, bytes_accessed=0, transcendentals=0),
        compiler_params=pltpu.CompilerParams(vmem_limit_bytes=16 << 20),
        name="early",
    )(time_steps, gathers, mate, split)
    other = swap(first, 1)
    spectra = []
    for i in range(inlines):
        spectra.append(
            pl.pallas_call(
                functools.partial(late_kernel, i),
                out_shape=jax.ShapeDtypeStruct((lines, 2 * bins, offsets), BF16),
                in_specs=[smem] + [vmem] * 5,
                out_specs=vmem,
                scratch_shapes=[
                    pltpu.VMEM((2, lines, offsets, depth), F32),
                    pltpu.VMEM((6, ROWS, depth), F32),
                    pltpu.VMEM((lines, offsets, depth), F32),
                ],
                cost_estimate=pl.CostEstimate(flops=3_000_000_000, bytes_accessed=0, transcendentals=0),
                compiler_params=pltpu.CompilerParams(vmem_limit_bytes=16 << 20),
            )(time_steps, halos[i], gathers, first if i < share else other, split, jnp.asarray(table))
        )
    rows = -(-inlines * lines // 16) * 16
    return pl.pallas_call(
        functools.partial(radon_kernel, near, apart, planes),
        out_shape=jax.ShapeDtypeStruct((inlines, lines, offsets, depth), BF16),
        in_specs=[vmem] * (len(spectra) + 5),
        out_specs=any_space,
        scratch_shapes=[
            pltpu.VMEM((rows * 2 * bins, offsets), F32),
            pltpu.VMEM((rows * 2 * bins, offsets), F32),
            pltpu.VMEM((inlines, lines, offsets, depth), BF16),
            pltpu.SemaphoreType.DMA((inlines, lines)),
        ],
        cost_estimate=pl.CostEstimate(flops=int(4e-6 * 1.0e15), bytes_accessed=0, transcendentals=0),
        compiler_params=pltpu.CompilerParams(vmem_limit_bytes=16 << 20),
        name="radon",
    )(*spectra, mine, theirs, mine_mate, theirs_mate, jnp.asarray(inverse_table(depth, bins)))


def solution(mesh):
    return jax.shard_map(
        swapped,
        mesh=mesh,
        in_specs=(P("parts", "xline", None, None), P(), P("xline", None, None, None)),
        out_specs=P("parts", "xline", None, None),
        check_vma=False,
    )
```
